128 devices in a mesh: aux: 16 (over y, z), ao: 8 (over x, core).
Axes of the slice: x: 4, y: 4, z: 4, core: 2. Of those that a mesh axis runs over, the one named last changes fastest.
Arguments:
- three_centre: bfloat16 [1024, 512, 1024], P('aux', 'ao'), may hold values from -6 to 6
- metric: bfloat16 [1024, 1024], P('aux'), may hold values from -0.1875 to 0.1875
- density: bfloat16 [512, 64], P('ao'), may hold values from -0.0009765625 to 0.0009765625
- schwarz: int32 [16, 8], P(None, 'ao'), may hold values 0 or 1
- density_pattern: int32 [32, 4], P('ao'), may hold values 0 or 1
- owner: int32 [16], replicated, may hold values from 0 to 15, as said below
Outputs:
- exchange_blocks: float32 [32, 4096], P('aux', 'ao')
The draws below stay inside these ranges and needn't reach their ends.
Inputs may be any that keep to these rules, and one draw needn't show every extreme that they name: No owner holds more than 2 row tiles, and some owner holds exactly 2. `schwarz`: 1 marks a significant tile. `density_pattern`: 1 marks a nonzero density sub-block.
All inputs are finite; a program needn't handle non-finite values. No bound on the sum of `schwarz` on one device may be relied on, other than what follows from the above.
Results may differ from the reference program's by a relative error of at most 0.0034.
Values may be sent and summed in bfloat16 or wider, within the bound.
A program may use at most 192 MiB of HBM per device.

```python
import jax
import jax.numpy as jnp
from jax import lax

TILE = 64
RT_DEV = 1
NAUX = 1024
CAP = 2
NRT = 16
NROW = 1024
NCT = 8
NCOL = 512
N_AUX = 16


def draw_owner(key, part):
    first_key, second_key, third_key = jax.random.split(key, 3)
    owner_count = NRT // RT_DEV
    slot_total = owner_count * CAP
    shuffled = jax.random.permutation(first_key, slot_total).astype(jnp.int32)
    slot_ids = jnp.arange(slot_total, dtype=jnp.int32)
    position = jnp.zeros((slot_total,), jnp.int32).at[shuffled].set(slot_ids)
    busiest = jax.random.randint(second_key, (), 0, owner_count).astype(jnp.int32)
    score = jnp.where(slot_ids // CAP == busiest, slot_ids % CAP, CAP + position)
    order_ids = jnp.argsort(score).astype(jnp.int32)
    chosen = order_ids[:NRT]
    tile_order = jax.random.permutation(third_key, NRT).astype(jnp.int32)
    return (chosen[tile_order] // CAP).astype(jnp.int32)


def place_ends(values, key, least, largest):
    shape = values.shape
    place = [jax.random.randint(jax.random.fold_in(key, axis), (), 0, shape[axis]) for axis in range(len(shape))]
    values = values.at[tuple(place)].set(least)
    longest = shape.index(max(shape))
    place[longest] = (place[longest] + 1) % shape[longest]
    return values.at[tuple(place)].set(largest)


def levels(key, extent, cuts, low, top_value):
    level = 1.0
    for axis_at, shards_of in cuts:
        steps = jax.random.uniform(jax.random.fold_in(jax.random.fold_in(key, 6), axis_at), (shards_of,), jnp.float32, low / len(cuts), top_value / len(cuts))
        level = level * jnp.repeat(jnp.exp(steps), extent[axis_at] // shards_of).reshape((-1,) + (1,) * (len(extent) - 1 - axis_at))
    return level


def centred(stream_key, extent, deviation, reach, pieces=(), kind=jnp.bfloat16):
    entries = deviation * jax.random.normal(stream_key, extent, jnp.float32)
    if pieces:
        entries = entries * levels(stream_key, extent, pieces, -0.22, 0.18)
    return jnp.clip(entries, -reach, reach).astype(kind)


def setup_inputs(seed: int = 0) -> dict:
    splits = jax.random.split(jax.random.key(seed), 7)
    three_centre = centred(splits[0], (NAUX, NCOL, NROW), 1.0, 6.0, ((0, 16), (1, 8)))
    metric = centred(splits[1], (NAUX, NAUX), NAUX ** -0.5, 0.1875, ((0, 16),))
    density = centred(splits[2], (NCOL, TILE), (TILE * TILE * NAUX * NCT) ** -0.5, 0.0009765625, ((0, 8),))
    schwarz = place_ends((jax.random.randint(splits[3], (NRT, NCT), 0, 4) < 3).astype(jnp.int32), jax.random.fold_in(splits[3], 1), 0, 1)
    density_pattern = place_ends((jax.random.randint(splits[4], (NCT * 4, 4), 0, 4) < 3).astype(jnp.int32), jax.random.fold_in(splits[4], 1), 0, 1)
    owner = draw_owner(jax.random.fold_in(splits[6], 71), 0)
    return {"three_centre": three_centre, "metric": metric, "density": density, "schwarz": schwarz, "density_pattern": density_pattern, "owner": owner}


def exchange_terms(fitted, masked_density):
    tile_size = masked_density.shape[0]
    group_count = fitted.shape[2] // tile_size
    mixed_terms = jnp.einsum("sl,qsm->qlm", masked_density.astype(jnp.float32), fitted.astype(jnp.float32)).astype(jnp.bfloat16)
    left_side = mixed_terms.reshape(-1, group_count, tile_size).astype(jnp.float32)
    right_side = fitted.reshape(-1, group_count, tile_size).astype(jnp.float32)
    blocks = jnp.einsum("xcm,xcn->cmn", left_side, right_side)
    return blocks.reshape(group_count, tile_size * tile_size)


def owner_targets(owner, capacity):
    tile_ids = jnp.arange(owner.shape[0], dtype=jnp.int32)
    same_owner = (owner[:, None] == owner[None, :]) & (tile_ids[None, :] < tile_ids[:, None])
    slot_index = jnp.sum(same_owner.astype(jnp.int32), axis=1).astype(jnp.int32)
    return (owner * capacity + slot_index).astype(jnp.int32)


def reference(three_centre, metric, density, schwarz, density_pattern, owner):
    tile_size = TILE
    sub_block = tile_size // 4
    keep_rows = jnp.repeat(schwarz, tile_size, axis=0)
    pattern = jnp.repeat(jnp.repeat(density_pattern, sub_block, axis=0), sub_block, axis=1)
    masked_density = density * pattern.astype(jnp.bfloat16)

    def one_slab(slab_index):
        slab_data = lax.dynamic_slice_in_dim(three_centre, slab_index * tile_size, tile_size, 1)
        keep_slab = lax.dynamic_slice_in_dim(keep_rows, slab_index, 1, 1)[:, 0].astype(jnp.bfloat16)
        screened = slab_data * keep_slab[None, None, :]
        fitted = jnp.dot(metric, screened.reshape(NAUX, -1), preferred_element_type=jnp.float32)
        fitted = fitted.astype(jnp.bfloat16).reshape(NAUX, tile_size, NROW)
        slab_density = lax.dynamic_slice_in_dim(masked_density, slab_index * tile_size, tile_size, 0)
        return exchange_terms(fitted, slab_density)

    per_slab = lax.map(one_slab, jnp.arange(NCT, dtype=jnp.int32))
    totals = jnp.sum(per_slab, axis=0)
    target = owner_targets(owner, CAP)
    result = jnp.zeros((N_AUX * CAP, tile_size * tile_size), jnp.float32)
    return result.at[target].set(totals)
```

```python
import jax
import jax.numpy as jnp
from jax import lax
from jax.experimental import pallas as pl
from jax.experimental.pallas import tpu as pltpu
from jax.sharding import PartitionSpec as P

MESH = pl.DeviceIdType.MESH
BF16 = jnp.bfloat16
F32 = jnp.float32

SIDE = 4
N_AUX = 16
N_AO = 8
TILE = 64
NAUX = 1024
PLOC = NAUX // N_AUX
CHUNKS = 8
AHEAD = 2
OFFSETS = (
    (0, 1), (1, 0), (0, 3), (3, 0), (1, 1), (3, 3), (0, 2), (2, 0),
    (1, 3), (3, 1), (1, 2), (2, 1), (3, 2), (2, 3), (2, 2),
)


def dot(a, b):
    return jnp.dot(a, b, preferred_element_type=F32)


def column_of(n):
    return 32 * ((n // 2) % 2) + 4 * (n // 8) + 2 * ((n // 4) % 2) + n % 2


def iota(shape, axis):
    return lax.broadcasted_iota(jnp.int32, shape, axis)


def kernel(
    x_ref, m_ref, d_ref, pat_ref, sch_ref, own_ref, o_ref,
    xs, sbuf, rbuf, gbuf, mfull, perm, wbuf, fbuf, kacc, kp, kr, kg,
    xsem, msem, lsem, ssem, rsem, m1s, m1r, m2s, m2r, k1s, k1r, k2s, k2r,
):
    me = lax.axis_index("aux")
    ao = lax.axis_index("ao")
    y, z = me // SIDE, me % SIDE
    px, core = ao // 2, ao % 2
    aux_peers = [((y + dy) % SIDE) * SIDE + (z + dz) % SIDE for dy, dz in OFFSETS]
    ao_peers = [(ao + k) % N_AO for k in range(1, N_AO)]

    def remote(src, dst, send_sem, recv_sem, aux, group):
        return pltpu.make_async_remote_copy(
            src_ref=src, dst_ref=dst, send_sem=send_sem, recv_sem=recv_sem,
            device_id=(aux, group), device_id_type=MESH,
        )

    def x_copy(half, h):
        rows = pl.ds(32 * h + 16 * half, 16)
        return pltpu.make_async_copy(x_ref.at[:, rows, :], xs.at[:, rows, :], xsem.at[half, h])

    for half in range(2):
        for h in range(2):
            x_copy(half, h).start()
    m_slot = mfull.at[core, pl.ds(pl.multiple_of(px * 256 + me * 16, 16), 16), :]
    m_copy = pltpu.make_async_copy(
        m_ref.at[pl.ds(pl.multiple_of(px * 16, 16), 16), pl.ds(pl.multiple_of(core * 512, 512), 512)],
        m_slot, msem,
    )
    m_copy.start()

    barrier = pltpu.get_barrier_semaphore()
    for peer in aux_peers:
        pl.semaphore_signal(barrier, inc=1, device_id=(peer, ao), device_id_type=MESH)
    for peer in ao_peers:
        pl.semaphore_signal(barrier, inc=1, device_id=(me, peer), device_id_type=MESH)

    row, col = iota((256, 256), 0), iota((256, 256), 1)
    perm[...] = jnp.where((row % 16) * 16 + row // 16 == col, 1.0, 0.0).astype(BF16)

    low = iota((256, 128), 1) < 64

    def pack(half):
        def one_pair(u, carry):
            lanes = pl.ds(pl.multiple_of(u * 128, 128), 128)
            for pb in range(PLOC // 16):
                prow = slice(16 * pb, 16 * pb + 16)
                blocks = [
                    xs[prow, pl.ds(32 * h + 16 * half, 16), lanes].reshape(256, 128)
                    for h in range(2)
                ]
                turned = dot(perm[...], jnp.concatenate(blocks, axis=1))
                first, second = turned[:, :128], turned[:, 128:]
                even = jnp.where(low, first, pltpu.roll(second, 64, 1)).astype(BF16)
                odd = jnp.where(low, pltpu.roll(first, 64, 1), second).astype(BF16)
                for which, value in enumerate((even, odd)):
                    value = value.reshape(4, 4, 16, 128)
                    for cc in range(4):
                        sbuf[4 * half + cc, 2 * u + which, :, prow, :] = value[cc]
            return carry

        lax.fori_loop(0, 8, one_pair, 0)

    def tile_copy(c, k):
        return remote(sbuf.at[c, aux_peers[k]], rbuf.at[c, me], ssem.at[c, k], rsem.at[c, k], aux_peers[k], ao)

    def own_copy(c):
        return pltpu.make_async_copy(sbuf.at[c, me], rbuf.at[c, me], lsem.at[c])

    def send(c):
        for k in range(len(OFFSETS)):
            tile_copy(c, k).start()
        own_copy(c).start()

    x_copy(0, 0).wait()
    x_copy(0, 1).wait()
    pack(0)
    m_copy.wait()
    pl.semaphore_wait(barrier, len(OFFSETS) + N_AO - 1)

    def m_first(k):
        return remote(m_slot, m_slot, m1s.at[k], m1r.at[k], aux_peers[k], ao)

    m_part = mfull.at[core, pl.ds(pl.multiple_of(px * 256, 256), 256), :]

    def m_second(k):
        return remote(m_part, m_part, m2s.at[k], m2r.at[k], me, ao_peers[k])

    for k in range(len(OFFSETS)):
        m_first(k).start()
    for c in range(AHEAD):
        send(c)
    x_copy(1, 0).wait()
    x_copy(1, 1).wait()
    pack(1)
    for k in range(len(OFFSETS)):
        m_first(k).wait_recv()
    for k in range(N_AO - 1):
        m_second(k).start()

    row, col = iota((TILE, TILE), 0), iota((TILE, TILE), 1)
    keep = jnp.zeros((TILE, TILE), jnp.int32)
    for i in range(4):
        for j in range(4):
            keep = keep + jnp.where((row // 16 == i) & (col // 16 == j), pat_ref[i, j], 0)
    masked = jnp.where(keep == 1, d_ref[...].astype(F32), 0.0).astype(BF16)
    spread = jnp.where(iota((TILE, 512), 0) == column_of(iota((TILE, 512), 1) // 8), 1.0, 0.0).astype(BF16)
    kacc[...] = jnp.zeros_like(kacc)

    def weights(c, carry):
        pick = jnp.where(
            iota((TILE, TILE), 1) == column_of(8 * c + iota((TILE, TILE), 0) // 8), 1.0, 0.0
        ).astype(BF16)
        upper = lax.dot_general(pick, masked, (((1,), (1,)), ((), ())), preferred_element_type=F32)
        lower = dot(pick, masked)
        both = dot(jnp.concatenate([upper, lower], axis=0).astype(BF16), spread)
        r, q = iota((128, 512), 0), iota((128, 512), 1)
        limit = jnp.where(r < 64, 8 * (c + 1), 8 * c)
        wbuf[c] = jnp.where((r % 8 == q % 8) & (q // 8 < limit), both, 0.0).astype(BF16)
        return carry

    lax.fori_loop(0, CHUNKS, weights, 0)

    def clear(b, carry):
        gbuf[b] = jnp.zeros((512, 128), BF16)
        return carry

    lax.fori_loop(0, 64, clear, 0)

    for k in range(N_AO - 1):
        m_second(k).wait_recv()

    low64 = iota((64, 128), 1) < 64

    def chunk(c, carry):
        @pl.when(c < CHUNKS - AHEAD)
        def _():
            send(c + AHEAD)

        for k in range(len(OFFSETS)):
            tile_copy(c, k).wait_recv()
        own_copy(c).wait()

        for jj in range(2):
            sides = [rbuf[c, :, 2 * jj + j, :, :].reshape(NAUX, 128) for j in range(2)]
            right = jnp.concatenate(sides, axis=1)
            fbuf[...] = dot(mfull[0], right[:512]) + dot(mfull[1], right[512:])

            def settle(b, inner):
                lo_rows = pl.ds(pl.multiple_of(b * 64, 64), 64)
                hi_rows = pl.ds(pl.multiple_of(512 + b * 64, 64), 64)
                sides = ([], [])
                for j in range(2):
                    lanes = slice(128 * j, 128 * j + 128)
                    lo, hi = fbuf[lo_rows, lanes], fbuf[hi_rows, lanes]
                    sides[0].append(jnp.where(low64, lo, pltpu.roll(hi, 64, 1)).reshape(8, 8, 128))
                    sides[1].append(jnp.where(low64, pltpu.roll(lo, 64, 1), hi).reshape(8, 8, 128))
                for h in range(2):
                    value = jnp.concatenate(sides[h], axis=1).astype(BF16)
                    at = pl.multiple_of(c * 64 + jj * 32 + h * 16, 16)
                    gbuf[pl.ds(b * 8, 8), pl.ds(at, 16), :] = value
                return inner

            lax.fori_loop(0, 8, settle, 0)

        weight = wbuf[c]

        def mix(b, inner):
            right = jnp.concatenate([gbuf[2 * b], gbuf[2 * b + 1]], axis=1)
            mixed = dot(weight, right).astype(BF16)
            at = pl.ds(pl.multiple_of(c * 64, 64), 64)
            n0, n1 = gbuf[2 * b, at, :], gbuf[2 * b + 1, at, :]
            left = jnp.concatenate([mixed[:64, :128], n0, mixed[:64, 128:], n1], axis=0)
            other = jnp.concatenate([n0, mixed[64:, :128], n1, mixed[64:, 128:]], axis=0)
            kacc[...] += lax.dot_general(left, other, (((0,), (0,)), ((), ())), preferred_element_type=F32)
            return inner

        lax.fori_loop(0, 32, mix, 0)
        return carry

    lax.fori_loop(0, CHUNKS, chunk, 0)

    total = kacc[:64, :] + pltpu.roll(kacc[64:, :], 64, 1)
    kp[...] = total * sch_ref[me, 0].astype(F32)

    def k_first(k):
        return remote(
            kp.at[pl.ds(pl.multiple_of(ao_peers[k] * 8, 8), 8), :], kr.at[ao],
            k1s.at[k], k1r.at[k], me, ao_peers[k],
        )

    def k_second(k):
        return remote(kg.at[me], kg.at[me], k2s.at[k], k2r.at[k], aux_peers[k], ao)

    for k in range(N_AO - 1):
        k_first(k).start()
    kr[ao] = kp[pl.ds(pl.multiple_of(ao * 8, 8), 8), :]
    for k in range(N_AO - 1):
        k_first(k).wait_recv()
    kg[me] = jnp.sum(kr[...], axis=0)
    for k in range(len(OFFSETS)):
        k_second(k).start()
    for k in range(len(OFFSETS)):
        k_second(k).wait_recv()

    picked = [jnp.zeros((8, 128), F32), jnp.zeros((8, 128), F32)]
    seen = jnp.int32(0)
    for t in range(N_AUX):
        hit = (own_ref[t] == me).astype(jnp.int32)
        for r in range(2):
            picked[r] = picked[r] + kg[t] * (hit * (seen == r).astype(jnp.int32)).astype(F32)
        seen = seen + hit
    low1 = iota((1, 128), 1) < 64
    for r in range(2):
        for k in range(4):
            even, odd = picked[r][2 * k : 2 * k + 1], picked[r][2 * k + 1 : 2 * k + 2]
            o_ref[r : r + 1, 128 * k : 128 * k + 128] = jnp.where(low1, even, pltpu.roll(odd, 64, 1))

    def drain(c, carry):
        for k in range(len(OFFSETS)):
            tile_copy(c, k).wait_send()
        return carry

    lax.fori_loop(0, CHUNKS, drain, 0)
    for k in range(len(OFFSETS)):
        m_first(k).wait_send()
        k_second(k).wait_send()
    for k in range(N_AO - 1):
        m_second(k).wait_send()
        k_first(k).wait_send()


def local(three_centre, metric, density, schwarz, density_pattern, owner):
    anywhere = pl.BlockSpec(memory_space=pl.ANY)
    vmem = pl.BlockSpec(memory_space=pltpu.VMEM)
    smem = pl.BlockSpec(memory_space=pltpu.SMEM)
    dma = pltpu.SemaphoreType.DMA
    n_off = len(OFFSETS)
    return pl.pallas_call(
        kernel,
        out_shape=jax.ShapeDtypeStruct((2, 512), F32),
        in_specs=[anywhere, anywhere, vmem, smem, smem, smem],
        out_specs=vmem,
        scratch_shapes=[
            pltpu.VMEM((PLOC, TILE, 1024), BF16),
            pltpu.VMEM((CHUNKS, N_AUX, 4, PLOC, 128), BF16),
            pltpu.VMEM((CHUNKS, N_AUX, 4, PLOC, 128), BF16),
            pltpu.VMEM((64, 512, 128), BF16),
            pltpu.VMEM((2, NAUX, 512), BF16),
            pltpu.VMEM((256, 256), BF16),
            pltpu.VMEM((CHUNKS, 128, 512), BF16),
            pltpu.VMEM((NAUX, 256), F32),
            pltpu.VMEM((128, 128), F32),
            pltpu.VMEM((64, 128), F32),
            pltpu.VMEM((N_AO, 8, 128), F32),
            pltpu.VMEM((N_AUX, 8, 128), F32),
            dma((2, 2)),
            dma,
            dma((CHUNKS,)),
            dma((CHUNKS, n_off)),
            dma((CHUNKS, n_off)),
            dma((n_off,)),
            dma((n_off,)),
            dma((N_AO - 1,)),
            dma((N_AO - 1,)),
            dma((N_AO - 1,)),
            dma((N_AO - 1,)),
            dma((n_off,)),
            dma((n_off,)),
        ],
        compiler_params=pltpu.CompilerParams(
            collective_id=0, has_side_effects=True, vmem_limit_bytes=56 * 2**20
        ),
    )(three_centre, metric, density, density_pattern, schwarz, owner)


def solution(mesh):
    return jax.shard_map(
        local,
        mesh=mesh,
        in_specs=(
            P("aux", "ao", None),
            P("aux", None),
            P("ao", None),
            P(None, "ao"),
            P("ao", None),
            P(),
        ),
        out_specs=P("aux", "ao"),
        check_vma=False,
    )
```

```python
import jax
import jax.numpy as jnp
from jax import lax
from jax.experimental import pallas as pl
from jax.experimental.pallas import tpu as pltpu
from jax.sharding import PartitionSpec as P

MESH = pl.DeviceIdType.MESH
BF16 = jnp.bfloat16
F32 = jnp.float32

SIDE = 4
N_AUX = 16
N_AO = 8
TILE = 64
NAUX = 1024
PLOC = NAUX // N_AUX
CHUNKS = 8
AHEAD = 6
STAGES = ((0, 4), (4, 6), (6, 7), (7, 8))
BLOCKS = 8
OFFSETS = (
    (0, 1), (1, 0), (0, 3), (3, 0), (1, 1), (3, 3), (0, 2), (2, 0),
    (1, 3), (3, 1), (1, 2), (2, 1), (3, 2), (2, 3), (2, 2),
)


def dot(a, b):
    return jnp.dot(a, b, preferred_element_type=F32)


def column_of(n):
    return 32 * ((n // 2) % 2) + 4 * (n // 8) + 2 * ((n // 4) % 2) + n % 2


def iota(shape, axis):
    return lax.broadcasted_iota(jnp.int32, shape, axis)


def kernel(
    x_ref, m_ref, d_ref, pat_ref, sch_ref, own_ref, o_ref,
    xs, sbuf, rbuf, gbuf, mfull, perm, wbuf, fbuf, kacc, kp, kr, kg,
    xsem, msem, lsem, ssem, rsem, m1s, m1r, m2s, m2r, k1s, k1r, k2s, k2r,
):
    me = lax.axis_index("aux")
    ao = lax.axis_index("ao")
    y, z = me // SIDE, me % SIDE
    px, core = ao // 2, ao % 2
    aux_peers = [((y + dy) % SIDE) * SIDE + (z + dz) % SIDE for dy, dz in OFFSETS]
    ao_peers = [(ao + k) % N_AO for k in range(1, N_AO)]

    def remote(src, dst, send_sem, recv_sem, aux, group):
        return pltpu.make_async_remote_copy(
            src_ref=src, dst_ref=dst, send_sem=send_sem, recv_sem=recv_sem,
            device_id=(aux, group), device_id_type=MESH,
        )

    def x_copy(half, h):
        rows = pl.ds(32 * h + 16 * half, 16)
        return pltpu.make_async_copy(x_ref.at[:, rows, :], xs.at[:, rows, :], xsem.at[half, h])

    for half in range(2):
        for h in range(2):
            x_copy(half, h).start()
    m_slot = mfull.at[core, pl.ds(pl.multiple_of(px * 256 + me * 16, 16), 16), :]
    m_copy = pltpu.make_async_copy(
        m_ref.at[pl.ds(pl.multiple_of(px * 16, 16), 16), pl.ds(pl.multiple_of(core * 512, 512), 512)],
        m_slot, msem,
    )
    m_copy.start()

    barrier = pltpu.get_barrier_semaphore()
    for peer in aux_peers:
        pl.semaphore_signal(barrier, inc=1, device_id=(peer, ao), device_id_type=MESH)
    for peer in ao_peers:
        pl.semaphore_signal(barrier, inc=1, device_id=(me, peer), device_id_type=MESH)

    row, col = iota((256, 256), 0), iota((256, 256), 1)
    perm[...] = jnp.where((row % 16) * 16 + row // 16 == col, 1.0, 0.0).astype(BF16)

    low = iota((256, 128), 1) < 64

    def pack(half):
        def one_pair(u, carry):
            lanes = pl.ds(pl.multiple_of(u * 128, 128), 128)
            for pb in range(PLOC // 16):
                prow = slice(16 * pb, 16 * pb + 16)
                blocks = [
                    xs[prow, pl.ds(32 * h + 16 * half, 16), lanes].reshape(256, 128)
                    for h in range(2)
                ]
                turned = dot(perm[...], jnp.concatenate(blocks, axis=1))
                first, second = turned[:, :128], turned[:, 128:]
                even = jnp.where(low, first, pltpu.roll(second, 64, 1)).astype(BF16)
                odd = jnp.where(low, pltpu.roll(first, 64, 1), second).astype(BF16)
                for which, value in enumerate((even, odd)):
                    value = value.reshape(4, 4, 16, 128)
                    for cc in range(4):
                        sbuf[4 * half + cc, 2 * u + which, :, prow, :] = value[cc]
            return carry

        lax.fori_loop(0, 8, one_pair, 0)

    def tile_copy(c, k):
        return remote(sbuf.at[c, aux_peers[k]], rbuf.at[c, me], ssem.at[c, k], rsem.at[c, k], aux_peers[k], ao)

    def own_copy(c):
        return pltpu.make_async_copy(sbuf.at[c, me], rbuf.at[c, me], lsem.at[c])

    def send(c):
        for k in range(len(OFFSETS)):
            tile_copy(c, k).start()
        own_copy(c).start()

    x_copy(0, 0).wait()
    x_copy(0, 1).wait()
    pack(0)
    m_copy.wait()
    pl.semaphore_wait(barrier, len(OFFSETS) + N_AO - 1)

    def m_first(k):
        return remote(m_slot, m_slot, m1s.at[k], m1r.at[k], aux_peers[k], ao)

    m_part = mfull.at[core, pl.ds(pl.multiple_of(px * 256, 256), 256), :]

    def m_second(k):
        return remote(m_part, m_part, m2s.at[k], m2r.at[k], me, ao_peers[k])

    for k in range(len(OFFSETS)):
        m_first(k).start()
    for c in range(1):
        send(c)
    x_copy(1, 0).wait()
    x_copy(1, 1).wait()
    pack(1)
    for k in range(len(OFFSETS)):
        m_first(k).wait_recv()
    for k in range(N_AO - 1):
        m_second(k).start()
    for c in range(1, AHEAD):
        send(c)

    row, col = iota((TILE, TILE), 0), iota((TILE, TILE), 1)
    keep = jnp.zeros((TILE, TILE), jnp.int32)
    for i in range(4):
        for j in range(4):
            keep = keep + jnp.where((row // 16 == i) & (col // 16 == j), pat_ref[i, j], 0)
    masked = jnp.where(keep == 1, d_ref[...].astype(F32), 0.0).astype(BF16)
    spread = jnp.where(iota((TILE, 512), 0) == column_of(iota((TILE, 512), 1) // 8), 1.0, 0.0).astype(BF16)
    kacc[...] = jnp.zeros_like(kacc)

    for stage, (lo, hi) in enumerate(STAGES):
        n_new = TILE * (hi - lo)
        pick = jnp.where(
            iota((n_new, TILE), 1) == column_of(8 * lo + iota((n_new, TILE), 0) // 8), 1.0, 0.0
        ).astype(BF16)
        parts = [lax.dot_general(pick, masked, (((1,), (1,)), ((), ())), preferred_element_type=F32)]
        if lo:
            parts.append(dot(pick, masked))
        for side, part in enumerate(parts):
            both = dot(part.astype(BF16), spread)
            r, q = iota((n_new, 512), 0), iota((n_new, 512), 1)
            limit = 8 * hi if side == 0 else 8 * lo
            wbuf[stage, side * n_new : (side + 1) * n_new, :] = jnp.where(
                (r % 8 == q % 8) & (q // 8 < limit), both, 0.0
            ).astype(BF16)

    def clear(b, carry):
        gbuf[b, 448:, :] = jnp.zeros((64, 128), BF16)
        return carry

    lax.fori_loop(0, 64, clear, 0)

    for k in range(N_AO - 1):
        m_second(k).wait_recv()

    low64 = iota((64, 128), 1) < 64

    def chunk(c, carry):
        @pl.when(c < CHUNKS - AHEAD)
        def _():
            send(c + AHEAD)

        for k in range(len(OFFSETS)):
            tile_copy(c, k).wait_recv()
        own_copy(c).wait()

        def fit(jj, middle):
            sides = [rbuf[c, :, 2 * jj + j, :, :].reshape(NAUX, 128) for j in range(2)]
            right = jnp.concatenate(sides, axis=1)
            fbuf[...] = dot(mfull[0], right[:512]) + dot(mfull[1], right[512:])

            def settle(b, inner):
                lo_rows = pl.ds(pl.multiple_of(b * 64, 64), 64)
                hi_rows = pl.ds(pl.multiple_of(512 + b * 64, 64), 64)
                sides = ([], [])
                for j in range(2):
                    lanes = slice(128 * j, 128 * j + 128)
                    lo, hi = fbuf[lo_rows, lanes], fbuf[hi_rows, lanes]
                    sides[0].append(jnp.where(low64, lo, pltpu.roll(hi, 64, 1)).reshape(8, 8, 128))
                    sides[1].append(jnp.where(low64, pltpu.roll(lo, 64, 1), hi).reshape(8, 8, 128))
                for h in range(2):
                    value = jnp.concatenate(sides[h], axis=1).astype(BF16)
                    at = pl.multiple_of(c * 64 + jj * 32 + h * 16, 16)
                    gbuf[pl.ds(b * 8, 8), pl.ds(at, 16), :] = value
                return inner

            lax.fori_loop(0, 8, settle, 0)
            return middle

        lax.fori_loop(0, 2, fit, 0)
        return carry

    def drain(c, carry):
        for k in range(len(OFFSETS)):
            tile_copy(c, k).wait_send()
        return carry

    for stage, (lo, hi) in enumerate(STAGES):
        if hi == CHUNKS:
            for k in range(len(OFFSETS)):
                m_first(k).wait_send()
            for k in range(N_AO - 1):
                m_second(k).wait_send()
            lax.fori_loop(0, lo, drain, 0)
        lax.fori_loop(lo, hi, chunk, 0)

        n_new = TILE * (hi - lo)
        depth = -(-TILE * hi // 128) * 128
        n_out = n_new * (2 if lo else 1)

        def mix(b, carry, stage=stage, lo=lo, n_new=n_new, depth=depth, n_out=n_out):
            blocks = [gbuf[BLOCKS * b + i, :depth, :] for i in range(BLOCKS)]
            mixed = dot(wbuf[stage, :n_out, :depth], jnp.concatenate(blocks, axis=1)).astype(BF16)
            left, other = [], []
            for i in range(BLOCKS):
                new = gbuf[BLOCKS * b + i, TILE * lo : TILE * lo + n_new, :]
                lanes = slice(128 * i, 128 * i + 128)
                left.append(mixed[:n_new, lanes])
                other.append(new)
                if lo:
                    left.append(new)
                    other.append(mixed[n_new:, lanes])
            kacc[...] += lax.dot_general(
                jnp.concatenate(left, axis=0), jnp.concatenate(other, axis=0),
                (((0,), (0,)), ((), ())), preferred_element_type=F32,
            )
            return carry

        lax.fori_loop(0, 64 // BLOCKS, mix, 0)

    total = kacc[:64, :] + pltpu.roll(kacc[64:, :], 64, 1)
    kp[...] = total * sch_ref[me].astype(F32)

    def k_first(k):
        return remote(
            kp.at[pl.ds(pl.multiple_of(ao_peers[k] * 8, 8), 8), :], kr.at[ao],
            k1s.at[k], k1r.at[k], me, ao_peers[k],
        )

    def k_second(k):
        return remote(kg.at[me], kg.at[me], k2s.at[k], k2r.at[k], aux_peers[k], ao)

    for k in range(N_AO - 1):
        k_first(k).start()
    kr[ao] = kp[pl.ds(pl.multiple_of(ao * 8, 8), 8), :]
    for k in range(N_AO - 1):
        k_first(k).wait_recv()
    kg[me] = jnp.sum(kr[...], axis=0)
    for k in range(len(OFFSETS)):
        k_second(k).start()
    for k in range(len(OFFSETS)):
        k_second(k).wait_recv()

    picked = [jnp.zeros((8, 128), F32), jnp.zeros((8, 128), F32)]
    seen = jnp.int32(0)
    for t in range(N_AUX):
        hit = (own_ref[t] == me).astype(jnp.int32)
        for r in range(2):
            picked[r] = picked[r] + kg[t] * (hit * (seen == r).astype(jnp.int32)).astype(F32)
        seen = seen + hit
    low1 = iota((1, 128), 1) < 64
    for r in range(2):
        for k in range(4):
            even, odd = picked[r][2 * k : 2 * k + 1], picked[r][2 * k + 1 : 2 * k + 2]
            o_ref[r : r + 1, 128 * k : 128 * k + 128] = jnp.where(low1, even, pltpu.roll(odd, 64, 1))

    for k in range(len(OFFSETS)):
        tile_copy(CHUNKS - 1, k).wait_send()
        k_second(k).wait_send()
    for k in range(N_AO - 1):
        k_first(k).wait_send()


def local(three_centre, metric, density, schwarz, density_pattern, owner):
    anywhere = pl.BlockSpec(memory_space=pl.ANY)
    vmem = pl.BlockSpec(memory_space=pltpu.VMEM)
    smem = pl.BlockSpec(memory_space=pltpu.SMEM)
    dma = pltpu.SemaphoreType.DMA
    n_off = len(OFFSETS)
    return pl.pallas_call(
        kernel,
        out_shape=jax.ShapeDtypeStruct((2, 512), F32),
        in_specs=[anywhere, anywhere, vmem, smem, smem, smem],
        out_specs=vmem,
        scratch_shapes=[
            pltpu.VMEM((PLOC, TILE, 1024), BF16),
            pltpu.VMEM((CHUNKS, N_AUX, 4, PLOC, 128), BF16),
            pltpu.VMEM((CHUNKS, N_AUX, 4, PLOC, 128), BF16),
            pltpu.VMEM((64, 512, 128), BF16),
            pltpu.VMEM((2, NAUX, 512), BF16),
            pltpu.VMEM((256, 256), BF16),
            pltpu.VMEM((len(STAGES), 256, 512), BF16),
            pltpu.VMEM((NAUX, 256), F32),
            pltpu.VMEM((128, 128), F32),
            pltpu.VMEM((64, 128), F32),
            pltpu.VMEM((N_AO, 8, 128), F32),
            pltpu.VMEM((N_AUX, 8, 128), F32),
            dma((2, 2)),
            dma,
            dma((CHUNKS,)),
            dma((CHUNKS, n_off)),
            dma((CHUNKS, n_off)),
            dma((n_off,)),
            dma((n_off,)),
            dma((N_AO - 1,)),
            dma((N_AO - 1,)),
            dma((N_AO - 1,)),
            dma((N_AO - 1,)),
            dma((n_off,)),
            dma((n_off,)),
        ],
        compiler_params=pltpu.CompilerParams(
            collective_id=0, has_side_effects=True, vmem_limit_bytes=56 * 2**20
        ),
    )(three_centre, metric, density, density_pattern, schwarz.reshape(N_AUX), owner)


def solution(mesh):
    return jax.shard_map(
        local,
        mesh=mesh,
        in_specs=(
            P("aux", "ao", None),
            P("aux", None),
            P("ao", None),
            P(None, "ao"),
            P("ao", None),
            P(),
        ),
        out_specs=P("aux", "ao"),
        check_vma=False,
    )
```

```python
import jax
import jax.numpy as jnp
from jax import lax
from jax.experimental import pallas as pl
from jax.experimental.pallas import tpu as pltpu
from jax.sharding import PartitionSpec as P

MESH = pl.DeviceIdType.MESH
BF16 = jnp.bfloat16
F32 = jnp.float32

SIDE = 4
N_AUX = 16
N_AO = 8
TILE = 64
NAUX = 1024
PLOC = NAUX // N_AUX
CHUNKS = 8
AHEAD = 6
STAGES = ((0, 4), (4, 7), (7, 8))
BLOCKS = 32
OFFSETS = (
    (0, 1), (1, 0), (0, 3), (3, 0), (1, 1), (3, 3), (0, 2), (2, 0),
    (1, 3), (3, 1), (1, 2), (2, 1), (3, 2), (2, 3), (2, 2),
)


def dot(a, b):
    return jnp.dot(a, b, preferred_element_type=F32)


def column_of(n):
    return 32 * ((n // 2) % 2) + 4 * (n // 8) + 2 * ((n // 4) % 2) + n % 2


def iota(shape, axis):
    return lax.broadcasted_iota(jnp.int32, shape, axis)


def kernel(
    x_ref, m_ref, d_in, pat_in, sch_in, own_in, o_ref,
    d_ref, pat_ref, sch_ref, own_ref, small_sem,
    xs, sbuf, rbuf, gbuf, mfull, perm, wbuf, fbuf, kacc, kp, kr, kg,
    xsem, msem, lsem, ssem, rsem, m1s, m1r, m2s, m2r, k1s, k1r, k2s, k2r,
):
    me = lax.axis_index("aux")
    ao = lax.axis_index("ao")
    y, z = me // SIDE, me % SIDE
    px, core = ao // 2, ao % 2
    aux_peers = [((y + dy) % SIDE) * SIDE + (z + dz) % SIDE for dy, dz in OFFSETS]
    ao_peers = [(ao + k) % N_AO for k in range(1, N_AO)]

    def remote(src, dst, send_sem, recv_sem, aux, group):
        return pltpu.make_async_remote_copy(
            src_ref=src, dst_ref=dst, send_sem=send_sem, recv_sem=recv_sem,
            device_id=(aux, group), device_id_type=MESH,
        )

    small = [
        pltpu.make_async_copy(src, dst, small_sem.at[i])
        for i, (src, dst) in enumerate(
            ((d_in, d_ref), (pat_in, pat_ref), (sch_in, sch_ref), (own_in, own_ref))
        )
    ]
    for copy in small:
        copy.start()

    def x_copy(half, h):
        rows = pl.ds(32 * h + 16 * half, 16)
        return pltpu.make_async_copy(x_ref.at[:, rows, :], xs.at[:, rows, :], xsem.at[half, h])

    for half in range(2):
        for h in range(2):
            x_copy(half, h).start()
    m_slot = mfull.at[core, pl.ds(pl.multiple_of(px * 256 + me * 16, 16), 16), :]
    m_copy = pltpu.make_async_copy(
        m_ref.at[pl.ds(pl.multiple_of(px * 16, 16), 16), pl.ds(pl.multiple_of(core * 512, 512), 512)],
        m_slot, msem,
    )
    m_copy.start()

    barrier = pltpu.get_barrier_semaphore()
    for peer in aux_peers:
        pl.semaphore_signal(barrier, inc=1, device_id=(peer, ao), device_id_type=MESH)
    for peer in ao_peers:
        pl.semaphore_signal(barrier, inc=1, device_id=(me, peer), device_id_type=MESH)

    row, col = iota((256, 256), 0), iota((256, 256), 1)
    perm[...] = jnp.where((row % 16) * 16 + row // 16 == col, 1.0, 0.0).astype(BF16)

    low = iota((256, 128), 1) < 64

    def pack(half):
        def one_pair(u, carry):
            lanes = pl.ds(pl.multiple_of(u * 128, 128), 128)
            for pb in range(PLOC // 16):
                prow = slice(16 * pb, 16 * pb + 16)
                blocks = [
                    xs[prow, pl.ds(32 * h + 16 * half, 16), lanes].reshape(256, 128)
                    for h in range(2)
                ]
                turned = dot(perm[...], jnp.concatenate(blocks, axis=1))
                first, second = turned[:, :128], turned[:, 128:]
                even = jnp.where(low, first, pltpu.roll(second, 64, 1)).astype(BF16)
                odd = jnp.where(low, pltpu.roll(first, 64, 1), second).astype(BF16)
                for which, value in enumerate((even, odd)):
                    value = value.reshape(4, 4, 16, 128)
                    for cc in range(4):
                        sbuf[4 * half + cc, 2 * u + which, :, prow, :] = value[cc]
            return carry

        lax.fori_loop(0, 8, one_pair, 0)

    def tile_copy(c, k):
        return remote(sbuf.at[c, aux_peers[k]], rbuf.at[c, me], ssem.at[c, k], rsem.at[c, k], aux_peers[k], ao)

    def own_copy(c):
        return pltpu.make_async_copy(sbuf.at[c, me], rbuf.at[c, me], lsem.at[c])

    def send(c):
        for k in range(len(OFFSETS)):
            tile_copy(c, k).start()
        own_copy(c).start()

    x_copy(0, 0).wait()
    x_copy(0, 1).wait()
    pack(0)
    m_copy.wait()
    pl.semaphore_wait(barrier, len(OFFSETS) + N_AO - 1)

    m_row = mfull.at[core, pl.ds(pl.multiple_of(px * 256 + y * 64, 64), 64), :]

    def m_first(k):
        return remote(m_slot, m_slot, m1s.at[k], m1r.at[k], y * SIDE + (z + k + 1) % SIDE, ao)

    def m_next(k):
        return remote(m_row, m_row, m1s.at[k + 3], m1r.at[k + 3], ((y + k + 1) % SIDE) * SIDE + z, ao)

    m_part = mfull.at[core, pl.ds(pl.multiple_of(px * 256, 256), 256), :]

    def m_second(k):
        return remote(m_part, m_part, m2s.at[k], m2r.at[k], me, ao_peers[k])

    for k in range(SIDE - 1):
        m_first(k).start()
    for c in range(1):
        send(c)
    x_copy(1, 0).wait()
    x_copy(1, 1).wait()
    for k in range(SIDE - 1):
        m_first(k).wait_recv()
    for k in range(SIDE - 1):
        m_next(k).start()
    pack(1)
    for k in range(SIDE - 1):
        m_next(k).wait_recv()
    for k in range(N_AO - 1):
        m_second(k).start()
    for c in range(1, AHEAD):
        send(c)

    for copy in small:
        copy.wait()
    row, col = iota((TILE, TILE), 0), iota((TILE, TILE), 1)
    keep = jnp.zeros((TILE, TILE), jnp.int32)
    for i in range(4):
        for j in range(4):
            keep = keep + jnp.where((row // 16 == i) & (col // 16 == j), pat_ref[i, j], 0)
    masked = jnp.where(keep == 1, d_ref[...].astype(F32), 0.0).astype(BF16)
    spread = jnp.where(iota((TILE, 512), 0) == column_of(iota((TILE, 512), 1) // 8), 1.0, 0.0).astype(BF16)
    kacc[...] = jnp.zeros_like(kacc)

    for stage, (lo, hi) in enumerate(STAGES):
        n_new = TILE * (hi - lo)
        pick = jnp.where(
            iota((n_new, TILE), 1) == column_of(8 * lo + iota((n_new, TILE), 0) // 8), 1.0, 0.0
        ).astype(BF16)
        parts = [lax.dot_general(pick, masked, (((1,), (1,)), ((), ())), preferred_element_type=F32)]
        if lo:
            parts.append(dot(pick, masked))
        for side, part in enumerate(parts):
            both = dot(part.astype(BF16), spread)
            r, q = iota((n_new, 512), 0), iota((n_new, 512), 1)
            limit = 8 * hi if side == 0 else 8 * lo
            wbuf[stage, side * n_new : (side + 1) * n_new, :] = jnp.where(
                (r % 8 == q % 8) & (q // 8 < limit), both, 0.0
            ).astype(BF16)

    def clear(b, carry):
        gbuf[b, 448:, :] = jnp.zeros((64, 128), BF16)
        return carry

    lax.fori_loop(0, 64, clear, 0)

    for k in range(N_AO - 1):
        m_second(k).wait_recv()

    low64 = iota((64, 128), 1) < 64

    def chunk(c, carry):
        @pl.when(c < CHUNKS - AHEAD)
        def _():
            send(c + AHEAD)

        for k in range(len(OFFSETS)):
            tile_copy(c, k).wait_recv()
        own_copy(c).wait()

        def fit(jj, middle):
            sides = [rbuf[c, :, 2 * jj + j, :, :].reshape(NAUX, 128) for j in range(2)]
            right = jnp.concatenate(sides, axis=1)
            fbuf[...] = dot(mfull[0], right[:512]) + dot(mfull[1], right[512:])

            def settle(b, inner):
                lo_rows = pl.ds(pl.multiple_of(b * 64, 64), 64)
                hi_rows = pl.ds(pl.multiple_of(512 + b * 64, 64), 64)
                sides = ([], [])
                for j in range(2):
                    lanes = slice(128 * j, 128 * j + 128)
                    lo, hi = fbuf[lo_rows, lanes], fbuf[hi_rows, lanes]
                    sides[0].append(jnp.where(low64, lo, pltpu.roll(hi, 64, 1)).reshape(8, 8, 128))
                    sides[1].append(jnp.where(low64, pltpu.roll(lo, 64, 1), hi).reshape(8, 8, 128))
                for h in range(2):
                    value = jnp.concatenate(sides[h], axis=1).astype(BF16)
                    at = pl.multiple_of(c * 64 + jj * 32 + h * 16, 16)
                    gbuf[pl.ds(b * 8, 8), pl.ds(at, 16), :] = value
                return inner

            lax.fori_loop(0, 8, settle, 0, unroll=True)
            return middle

        lax.fori_loop(0, 2, fit, 0)
        return carry

    def drain(c, carry):
        for k in range(len(OFFSETS)):
            tile_copy(c, k).wait_send()
        return carry

    for stage, (lo, hi) in enumerate(STAGES):
        if hi == CHUNKS:
            for k in range(SIDE - 1):
                m_first(k).wait_send()
                m_next(k).wait_send()
            for k in range(N_AO - 1):
                m_second(k).wait_send()
            lax.fori_loop(0, lo, drain, 0)
        lax.fori_loop(lo, hi, chunk, 0)

        n_new = TILE * (hi - lo)
        depth = -(-TILE * hi // 128) * 128
        n_out = n_new * (2 if lo else 1)

        def mix(b, carry, stage=stage, lo=lo, n_new=n_new, depth=depth, n_out=n_out):
            blocks = [gbuf[BLOCKS * b + i, :depth, :] for i in range(BLOCKS)]
            mixed = dot(wbuf[stage, :n_out, :depth], jnp.concatenate(blocks, axis=1)).astype(BF16)
            left, other = [], []
            for i in range(BLOCKS):
                new = gbuf[BLOCKS * b + i, TILE * lo : TILE * lo + n_new, :]
                lanes = slice(128 * i, 128 * i + 128)
                left.append(mixed[:n_new, lanes])
                other.append(new)
                if lo:
                    left.append(new)
                    other.append(mixed[n_new:, lanes])
            kacc[...] += lax.dot_general(
                jnp.concatenate(left, axis=0), jnp.concatenate(other, axis=0),
                (((0,), (0,)), ((), ())), preferred_element_type=F32,
            )
            return carry

        lax.fori_loop(0, 64 // BLOCKS, mix, 0)

    total = kacc[:64, :] + pltpu.roll(kacc[64:, :], 64, 1)
    kp[...] = total * sch_ref[me].astype(F32)

    def k_first(k):
        return remote(
            kp.at[pl.ds(pl.multiple_of(ao_peers[k] * 8, 8), 8), :], kr.at[ao],
            k1s.at[k], k1r.at[k], me, ao_peers[k],
        )

    def k_second(k):
        return remote(kg.at[me], kg.at[me], k2s.at[k], k2r.at[k], aux_peers[k], ao)

    for k in range(N_AO - 1):
        k_first(k).start()
    kr[ao] = kp[pl.ds(pl.multiple_of(ao * 8, 8), 8), :]
    for k in range(N_AO - 1):
        k_first(k).wait_recv()
    kg[me] = jnp.sum(kr[...], axis=0)
    for k in range(len(OFFSETS)):
        k_second(k).start()
    for k in range(len(OFFSETS)):
        k_second(k).wait_recv()

    picked = [jnp.zeros((8, 128), F32), jnp.zeros((8, 128), F32)]
    seen = jnp.int32(0)
    for t in range(N_AUX):
        hit = (own_ref[t] == me).astype(jnp.int32)
        for r in range(2):
            picked[r] = picked[r] + kg[t] * (hit * (seen == r).astype(jnp.int32)).astype(F32)
        seen = seen + hit
    low1 = iota((1, 128), 1) < 64
    for r in range(2):
        for k in range(4):
            even, odd = picked[r][2 * k : 2 * k + 1], picked[r][2 * k + 1 : 2 * k + 2]
            o_ref[r : r + 1, 128 * k : 128 * k + 128] = jnp.where(low1, even, pltpu.roll(odd, 64, 1))

    for k in range(len(OFFSETS)):
        tile_copy(CHUNKS - 1, k).wait_send()
        k_second(k).wait_send()
    for k in range(N_AO - 1):
        k_first(k).wait_send()


def local(three_centre, metric, density, schwarz, density_pattern, owner):
    anywhere = pl.BlockSpec(memory_space=pl.ANY)
    vmem = pl.BlockSpec(memory_space=pltpu.VMEM)
    dma = pltpu.SemaphoreType.DMA
    n_off = len(OFFSETS)
    return pl.pallas_call(
        kernel,
        out_shape=jax.ShapeDtypeStruct((2, 512), F32),
        in_specs=[anywhere] * 6,
        out_specs=vmem,
        scratch_shapes=[
            pltpu.VMEM((TILE, TILE), BF16),
            pltpu.SMEM((4, 4), jnp.int32),
            pltpu.SMEM((N_AUX,), jnp.int32),
            pltpu.SMEM((N_AUX,), jnp.int32),
            dma((4,)),
            pltpu.VMEM((PLOC, TILE, 1024), BF16),
            pltpu.VMEM((CHUNKS, N_AUX, 4, PLOC, 128), BF16),
            pltpu.VMEM((CHUNKS, N_AUX, 4, PLOC, 128), BF16),
            pltpu.VMEM((64, 512, 128), BF16),
            pltpu.VMEM((2, NAUX, 512), BF16),
            pltpu.VMEM((256, 256), BF16),
            pltpu.VMEM((len(STAGES), 384, 512), BF16),
            pltpu.VMEM((NAUX, 256), F32),
            pltpu.VMEM((128, 128), F32),
            pltpu.VMEM((64, 128), F32),
            pltpu.VMEM((N_AO, 8, 128), F32),
            pltpu.VMEM((N_AUX, 8, 128), F32),
            dma((2, 2)),
            dma,
            dma((CHUNKS,)),
            dma((CHUNKS, n_off)),
            dma((CHUNKS, n_off)),
            dma((2 * SIDE - 2,)),
            dma((2 * SIDE - 2,)),
            dma((N_AO - 1,)),
            dma((N_AO - 1,)),
            dma((N_AO - 1,)),
            dma((N_AO - 1,)),
            dma((n_off,)),
            dma((n_off,)),
        ],
        compiler_params=pltpu.CompilerParams(
            collective_id=0, has_side_effects=True, vmem_limit_bytes=56 * 2**20
        ),
    )(three_centre, metric, density, density_pattern, schwarz.reshape(N_AUX), owner)


def solution(mesh):
    return jax.shard_map(
        local,
        mesh=mesh,
        in_specs=(
            P("aux", "ao", None),
            P("aux", None),
            P("ao", None),
            P(None, "ao"),
            P("ao", None),
            P(),
        ),
        out_specs=P("aux", "ao"),
        check_vma=False,
    )
```

```python
import jax
import jax.numpy as jnp
from jax import lax
from jax.experimental import pallas as pl
from jax.experimental.pallas import tpu as pltpu
from jax.sharding import PartitionSpec as P

MESH = pl.DeviceIdType.MESH
BF16 = jnp.bfloat16
F32 = jnp.float32

SIDE = 4
N_AUX = 16
N_AO = 8
TILE = 64
NAUX = 1024
PLOC = NAUX // N_AUX
CHUNKS = 8
AHEAD = 6
STAGES = ((0, 4), (4, 7), (7, 8))
BLOCKS = 32
OFFSETS = (
    (0, 1), (1, 0), (0, 3), (3, 0), (1, 1), (3, 3), (0, 2), (2, 0),
    (1, 3), (3, 1), (1, 2), (2, 1), (3, 2), (2, 3), (2, 2),
)


def dot(a, b):
    return jnp.dot(a, b, preferred_element_type=F32)


def column_of(n):
    return 32 * ((n // 2) % 2) + 4 * (n // 8) + 2 * ((n // 4) % 2) + n % 2


def iota(shape, axis):
    return lax.broadcasted_iota(jnp.int32, shape, axis)


def kernel(
    x_ref, m_ref, d_in, pat_in, sch_in, own_in, o_ref,
    d_ref, pat_ref, sch_ref, own_ref, small_sem,
    xs, sbuf, rbuf, gbuf, mfull, perm, wbuf, fbuf, kacc, kp, kr, kg,
    xsem, msem, lsem, ssem, rsem, m1s, m1r, m2s, m2r, k1s, k1r, k2s, k2r,
):
    me = lax.axis_index("aux")
    ao = lax.axis_index("ao")
    y, z = me // SIDE, me % SIDE
    px, core = ao // 2, ao % 2
    aux_peers = [((y + dy) % SIDE) * SIDE + (z + dz) % SIDE for dy, dz in OFFSETS]
    ao_peers = [(ao + k) % N_AO for k in range(1, N_AO)]

    def remote(src, dst, send_sem, recv_sem, aux, group):
        return pltpu.make_async_remote_copy(
            src_ref=src, dst_ref=dst, send_sem=send_sem, recv_sem=recv_sem,
            device_id=(aux, group), device_id_type=MESH,
        )

    small = [
        pltpu.make_async_copy(src, dst, small_sem.at[i])
        for i, (src, dst) in enumerate(
            ((d_in, d_ref), (pat_in, pat_ref), (sch_in, sch_ref), (own_in, own_ref))
        )
    ]
    for copy in small:
        copy.start()

    def x_copy(half, h):
        rows = pl.ds(32 * h + 16 * half, 16)
        return pltpu.make_async_copy(x_ref.at[:, rows, :], xs.at[:, rows, :], xsem.at[half, h])

    for half in range(2):
        for h in range(2):
            x_copy(half, h).start()
    m_slot = mfull.at[core, pl.ds(pl.multiple_of(px * 256 + me * 16, 16), 16), :]
    m_copy = pltpu.make_async_copy(
        m_ref.at[pl.ds(pl.multiple_of(px * 16, 16), 16), pl.ds(pl.multiple_of(core * 512, 512), 512)],
        m_slot, msem,
    )
    m_copy.start()

    barrier = pltpu.get_barrier_semaphore()
    for peer in aux_peers:
        pl.semaphore_signal(barrier, inc=1, device_id=(peer, ao), device_id_type=MESH)
    for peer in ao_peers:
        pl.semaphore_signal(barrier, inc=1, device_id=(me, peer), device_id_type=MESH)

    row, col = iota((256, 256), 0), iota((256, 256), 1)
    perm[...] = jnp.where((row % 16) * 16 + row // 16 == col, 1.0, 0.0).astype(BF16)

    low = iota((256, 128), 1) < 64

    def pack(half):
        def one_pair(u, carry):
            lanes = pl.ds(pl.multiple_of(u * 128, 128), 128)
            for pb in range(PLOC // 16):
                prow = slice(16 * pb, 16 * pb + 16)
                blocks = [
                    xs[prow, pl.ds(32 * h + 16 * half, 16), lanes].reshape(256, 128)
                    for h in range(2)
                ]
                turned = dot(perm[...], jnp.concatenate(blocks, axis=1))
                first, second = turned[:, :128], turned[:, 128:]
                even = jnp.where(low, first, pltpu.roll(second, 64, 1)).astype(BF16)
                odd = jnp.where(low, pltpu.roll(first, 64, 1), second).astype(BF16)
                for which, value in enumerate((even, odd)):
                    value = value.reshape(4, 4, 16, 128)
                    for cc in range(4):
                        sbuf[4 * half + cc, 2 * u + which, :, prow, :] = value[cc]
            return carry

        lax.fori_loop(0, 8, one_pair, 0)

    def tile_copy(c, k):
        return remote(sbuf.at[c, aux_peers[k]], rbuf.at[c, me], ssem.at[c, k], rsem.at[c, k], aux_peers[k], ao)

    def own_copy(c):
        return pltpu.make_async_copy(sbuf.at[c, me], rbuf.at[c, me], lsem.at[c])

    def send(c):
        for k in range(len(OFFSETS)):
            tile_copy(c, k).start()
        own_copy(c).start()

    x_copy(0, 0).wait()
    x_copy(0, 1).wait()
    pack(0)
    m_copy.wait()
    pl.semaphore_wait(barrier, len(OFFSETS) + N_AO - 1)

    m_row = mfull.at[core, pl.ds(pl.multiple_of(px * 256 + y * 64, 64), 64), :]

    def m_first(k):
        return remote(m_slot, m_slot, m1s.at[k], m1r.at[k], y * SIDE + (z + k + 1) % SIDE, ao)

    def m_next(k):
        return remote(m_row, m_row, m1s.at[k + 3], m1r.at[k + 3], ((y + k + 1) % SIDE) * SIDE + z, ao)

    m_part = mfull.at[core, pl.ds(pl.multiple_of(px * 256, 256), 256), :]

    def m_second(k):
        return remote(m_part, m_part, m2s.at[k], m2r.at[k], me, ao_peers[k])

    for k in range(SIDE - 1):
        m_first(k).start()
    for c in range(1):
        send(c)
    x_copy(1, 0).wait()
    x_copy(1, 1).wait()
    for k in range(SIDE - 1):
        m_first(k).wait_recv()
    for k in range(SIDE - 1):
        m_next(k).start()
    pack(1)
    for k in range(SIDE - 1):
        m_next(k).wait_recv()
    for k in range(N_AO - 1):
        m_second(k).start()
    for c in range(1, AHEAD):
        send(c)

    for copy in small:
        copy.wait()
    row, col = iota((TILE, TILE), 0), iota((TILE, TILE), 1)
    keep = jnp.zeros((TILE, TILE), jnp.int32)
    for i in range(4):
        for j in range(4):
            keep = keep + jnp.where((row // 16 == i) & (col // 16 == j), pat_ref[i, j], 0)
    masked = jnp.where(keep == 1, d_ref[...].astype(F32), 0.0).astype(BF16)
    spread = jnp.where(iota((TILE, 512), 0) == column_of(iota((TILE, 512), 1) // 8), 1.0, 0.0).astype(BF16)
    kacc[...] = jnp.zeros_like(kacc)

    for stage, (lo, hi) in enumerate(STAGES):
        n_new = TILE * (hi - lo)
        pick = jnp.where(
            iota((n_new, TILE), 1) == column_of(8 * lo + iota((n_new, TILE), 0) // 8), 1.0, 0.0
        ).astype(BF16)
        parts = [lax.dot_general(pick, masked, (((1,), (1,)), ((), ())), preferred_element_type=F32)]
        if lo:
            parts.append(dot(pick, masked))
        for side, part in enumerate(parts):
            both = dot(part.astype(BF16), spread)
            r, q = iota((n_new, 512), 0), iota((n_new, 512), 1)
            limit = 8 * hi if side == 0 else 8 * lo
            wbuf[stage, side * n_new : (side + 1) * n_new, :] = jnp.where(
                (r % 8 == q % 8) & (q // 8 < limit), both, 0.0
            ).astype(BF16)

    def clear(b, carry):
        gbuf[b, 448:, :] = jnp.zeros((64, 128), BF16)
        return carry

    lax.fori_loop(0, 64, clear, 0)

    for k in range(N_AO - 1):
        m_second(k).wait_recv()

    low64 = iota((64, 128), 1) < 64

    def chunk(c, carry):
        @pl.when(c < CHUNKS - AHEAD)
        def _():
            send(c + AHEAD)

        for k in range(len(OFFSETS)):
            tile_copy(c, k).wait_recv()
        own_copy(c).wait()

        def fit(jj, middle):
            sides = [rbuf[c, :, 2 * jj + j, :, :].reshape(NAUX, 128) for j in range(2)]
            right = jnp.concatenate(sides, axis=1)
            fbuf[...] = dot(mfull[0], right[:512]) + dot(mfull[1], right[512:])

            def settle(b, inner):
                lo_rows = pl.ds(pl.multiple_of(b * 64, 64), 64)
                hi_rows = pl.ds(pl.multiple_of(512 + b * 64, 64), 64)
                sides = ([], [])
                for j in range(2):
                    lanes = slice(128 * j, 128 * j + 128)
                    lo, hi = fbuf[lo_rows, lanes], fbuf[hi_rows, lanes]
                    sides[0].append(jnp.where(low64, lo, pltpu.roll(hi, 64, 1)).reshape(8, 8, 128))
                    sides[1].append(jnp.where(low64, pltpu.roll(lo, 64, 1), hi).reshape(8, 8, 128))
                for h in range(2):
                    value = jnp.concatenate(sides[h], axis=1).astype(BF16)
                    at = pl.multiple_of(c * 64 + jj * 32 + h * 16, 16)
                    gbuf[pl.ds(b * 8, 8), pl.ds(at, 16), :] = value
                return inner

            lax.fori_loop(0, 8, settle, 0, unroll=True)
            return middle

        lax.fori_loop(0, 2, fit, 0)
        return carry

    def drain(c, carry):
        for k in range(len(OFFSETS)):
            tile_copy(c, k).wait_send()
        return carry

    for stage, (lo, hi) in enumerate(STAGES):
        if hi == CHUNKS:
            for k in range(SIDE - 1):
                m_first(k).wait_send()
                m_next(k).wait_send()
            for k in range(N_AO - 1):
                m_second(k).wait_send()
            lax.fori_loop(0, lo, drain, 0)
        lax.fori_loop(lo, hi, chunk, 0)

        n_new = TILE * (hi - lo)
        depth = -(-TILE * hi // 128) * 128
        n_out = n_new * (2 if lo else 1)

        def mix(b, carry, stage=stage, lo=lo, n_new=n_new, depth=depth, n_out=n_out):
            blocks = [gbuf[BLOCKS * b + i, :depth, :] for i in range(BLOCKS)]
            mixed = dot(wbuf[stage, :n_out, :depth], jnp.concatenate(blocks, axis=1)).astype(BF16)
            left, other = [], []
            for i in range(BLOCKS):
                new = gbuf[BLOCKS * b + i, TILE * lo : TILE * lo + n_new, :]
                lanes = slice(128 * i, 128 * i + 128)
                left.append(mixed[:n_new, lanes])
                other.append(new)
                if lo:
                    left.append(new)
                    other.append(mixed[n_new:, lanes])
            kacc[...] += lax.dot_general(
                jnp.concatenate(left, axis=0), jnp.concatenate(other, axis=0),
                (((0,), (0,)), ((), ())), preferred_element_type=F32,
            )
            return carry

        lax.fori_loop(0, 64 // BLOCKS, mix, 0)

    total = kacc[:64, :] + pltpu.roll(kacc[64:, :], 64, 1)
    kp[...] = total * sch_ref[me].astype(F32)

    def k_first(k):
        return remote(
            kp.at[pl.ds(pl.multiple_of(ao_peers[k] * 8, 8), 8), :], kr.at[ao],
            k1s.at[k], k1r.at[k], me, ao_peers[k],
        )

    def k_second(k):
        return remote(kg.at[me], kg.at[me], k2s.at[k], k2r.at[k], aux_peers[k], ao)

    for k in (3, 2, 4, 1, 5, 0, 6):
        k_first(k).start()
    kr[ao] = kp[pl.ds(pl.multiple_of(ao * 8, 8), 8), :]
    for k in range(N_AO - 1):
        k_first(k).wait_recv()
    kg[me] = jnp.sum(kr[...], axis=0)
    for k in reversed(range(len(OFFSETS))):
        k_second(k).start()
    for k in range(len(OFFSETS)):
        k_second(k).wait_recv()

    picked = [jnp.zeros((8, 128), F32), jnp.zeros((8, 128), F32)]
    seen = jnp.int32(0)
    for t in range(N_AUX):
        hit = (own_ref[t] == me).astype(jnp.int32)
        for r in range(2):
            picked[r] = picked[r] + kg[t] * (hit * (seen == r).astype(jnp.int32)).astype(F32)
        seen = seen + hit
    low1 = iota((1, 128), 1) < 64
    for r in range(2):
        for k in range(4):
            even, odd = picked[r][2 * k : 2 * k + 1], picked[r][2 * k + 1 : 2 * k + 2]
            o_ref[r : r + 1, 128 * k : 128 * k + 128] = jnp.where(low1, even, pltpu.roll(odd, 64, 1))

    for k in range(len(OFFSETS)):
        tile_copy(CHUNKS - 1, k).wait_send()
        k_second(k).wait_send()
    for k in range(N_AO - 1):
        k_first(k).wait_send()


def local(three_centre, metric, density, schwarz, density_pattern, owner):
    anywhere = pl.BlockSpec(memory_space=pl.ANY)
    vmem = pl.BlockSpec(memory_space=pltpu.VMEM)
    dma = pltpu.SemaphoreType.DMA
    n_off = len(OFFSETS)
    return pl.pallas_call(
        kernel,
        out_shape=jax.ShapeDtypeStruct((2, 512), F32),
        in_specs=[anywhere] * 6,
        out_specs=vmem,
        scratch_shapes=[
            pltpu.VMEM((TILE, TILE), BF16),
            pltpu.SMEM((4, 4), jnp.int32),
            pltpu.SMEM((N_AUX,), jnp.int32),
            pltpu.SMEM((N_AUX,), jnp.int32),
            dma((4,)),
            pltpu.VMEM((PLOC, TILE, 1024), BF16),
            pltpu.VMEM((CHUNKS, N_AUX, 4, PLOC, 128), BF16),
            pltpu.VMEM((CHUNKS, N_AUX, 4, PLOC, 128), BF16),
            pltpu.VMEM((64, 512, 128), BF16),
            pltpu.VMEM((2, NAUX, 512), BF16),
            pltpu.VMEM((256, 256), BF16),
            pltpu.VMEM((len(STAGES), 384, 512), BF16),
            pltpu.VMEM((NAUX, 256), F32),
            pltpu.VMEM((128, 128), F32),
            pltpu.VMEM((64, 128), F32),
            pltpu.VMEM((N_AO, 8, 128), F32),
            pltpu.VMEM((N_AUX, 8, 128), F32),
            dma((2, 2)),
            dma,
            dma((CHUNKS,)),
            dma((CHUNKS, n_off)),
            dma((CHUNKS, n_off)),
            dma((2 * SIDE - 2,)),
            dma((2 * SIDE - 2,)),
            dma((N_AO - 1,)),
            dma((N_AO - 1,)),
            dma((N_AO - 1,)),
            dma((N_AO - 1,)),
            dma((n_off,)),
            dma((n_off,)),
        ],
        compiler_params=pltpu.CompilerParams(
            collective_id=0, has_side_effects=True, vmem_limit_bytes=56 * 2**20
        ),
    )(three_centre, metric, density, density_pattern, schwarz.reshape(N_AUX), owner)


def solution(mesh):
    return jax.shard_map(
        local,
        mesh=mesh,
        in_specs=(
            P("aux", "ao", None),
            P("aux", None),
            P("ao", None),
            P(None, "ao"),
            P("ao", None),
            P(),
        ),
        out_specs=P("aux", "ao"),
        check_vma=False,
    )
```
